512 devices in a mesh: imp: 32 (over z, x), adv: 16 (over y, core).
Axes of the slice: x: 4, y: 8, z: 8, core: 2. Of those that a mesh axis runs over, the one named last changes fastest.
Arguments:
- impression_vectors: bfloat16 [64, 65536], P(None, 'imp'), may hold values from -6 to 6
- advertiser_vectors: bfloat16 [64, 65536], P(None, ('imp', 'adv')), may hold values from -0.75 to 0.75
- spend_limits: float32 [65536], P(('imp', 'adv')), may hold values from 1024 to 8192
- capacity: float32 [65536], P('imp'), may hold values from 1024 to 8192
- blocks: int32 [512, 16, 8], P('imp', 'adv'), may hold values from 0 to 511, as said below
- counts: int32 [512, 16], P('imp', 'adv'), may hold values from 1 to 8, as said below
Outputs:
- prices: float32 [65536], P(('imp', 'adv'))
- impression_duals: float32 [65536], P('imp')
- impression_grad: bfloat16 [64, 65536], P(None, ('imp', 'adv'))
- advertiser_grad: bfloat16 [64, 65536], P(None, ('imp', 'adv'))
The draws below stay inside these ranges and needn't reach their ends.
Inputs may be any that keep to these rules, and one draw needn't show every extreme that they name: Block numbers. Entry [g, a, k] names a block b with (b) % (the size of adv) == a. The 8 entries of one list are distinct; entries at slots k >= counts[g, a] are padding and name valid blocks too. `counts`: every group has one index of adv whose count is 8.
All inputs are finite; a program needn't handle non-finite values.
Results may differ from the reference program's by a relative error of at most 0.012.
Values may be sent and summed in bfloat16 or wider, within the bound.
No kernel may reach another device: no remote copies, remote signals or barrier semaphores. Data moves between devices by JAX's collectives and lax.ppermute only.
A program may use at most 64 MiB of HBM per device.

```python
import math
import jax
import jax.numpy as jnp
from jax import lax

E = 64
GROUP = 128
BLOCK = 128
K = 8
ITERS = 3
BLK_DEV = 1
GROUPS = 512
IMPRESSIONS = 65536
ADV = 65536
N_IMP = 32
N_ADV = 16


def draw_blocks(key, part):
    served = BLK_DEV * N_IMP
    scores = jax.random.randint(key, (GROUPS, N_ADV, served), 0, 1 << 20) * served + jnp.arange(served)
    ranking = jnp.argsort(scores, axis=-1, stable=True)[..., :K]
    holder = ranking // BLK_DEV
    inside = ranking % BLK_DEV
    owning = jnp.arange(N_ADV)[None, :, None]
    return ((holder * N_ADV + owning) * BLK_DEV + inside).astype(jnp.int32)


def draw_counts(key, part):
    first_key, second_key, third_key = jax.random.split(jax.random.fold_in(key, 7), 3)
    first = jax.random.randint(first_key, (GROUPS, N_ADV), 1, K + 1)
    second = jax.random.randint(second_key, (GROUPS, N_ADV), 1, K + 1)
    lesser = jnp.minimum(first, second)
    anchor = jax.random.randint(third_key, (GROUPS, 1), 0, N_ADV)
    return jnp.where(jnp.arange(N_ADV)[None, :] == anchor, K, lesser).astype(jnp.int32)


def block_levels(rng, shape, cuts, smallest, high):
    level, own = 1.0, jax.random.fold_in(rng, 6)
    for dim, shards_of in cuts:
        heights = jnp.exp(jax.random.uniform(jax.random.fold_in(own, dim), (shards_of,), jnp.float32, smallest / len(cuts), high / len(cuts)))
        level = level * jnp.repeat(heights, shape[dim] // shards_of).reshape([-1 if axis == dim else 1 for axis in range(len(shape))])
    return level


def scatter_about(stream_key, shape, deviation, reach, cuts=(), held_as=jnp.bfloat16):
    drawn = jax.random.normal(stream_key, shape, jnp.float32) * deviation
    if len(cuts) > 0:
        drawn = block_levels(stream_key, shape, cuts, -0.22, 0.18) * drawn
    return jnp.clip(drawn, min=-reach, max=reach).astype(held_as)


def setup_inputs(seed: int = 0) -> dict:
    splits = jax.random.split(jax.random.key(seed), 7)
    return {
        "impression_vectors": scatter_about(splits[0], (E, IMPRESSIONS), 1.0, 6.0, ((1, 32),)),
        "advertiser_vectors": scatter_about(splits[1], (E, ADV), E ** -0.5, 0.75, ((1, 512),)),
        "spend_limits": jnp.clip(jnp.exp(math.log(8192.0) - 2.0794415 * jax.random.uniform(splits[2], (ADV,), jnp.float32) ** block_levels(splits[2], (ADV,), ((0, 512),), -0.2, 0.2)), 1024.0, 8192.0),
        "capacity": jnp.clip(jnp.exp(math.log(8192.0) - 2.0794415 * jax.random.uniform(splits[3], (IMPRESSIONS,), jnp.float32) ** block_levels(splits[3], (IMPRESSIONS,), ((0, 32),), -0.2, 0.2)), 1024.0, 8192.0),
        "blocks": draw_blocks(jax.random.fold_in(splits[6], 71), 0),
        "counts": draw_counts(jax.random.fold_in(splits[6], 71), 0),
    }


def reference(impression_vectors, advertiser_vectors, spend_limits, capacity, blocks, counts):
    groups = blocks.shape[0]
    features = impression_vectors.shape[0]
    block_total = advertiser_vectors.shape[1] // BLOCK
    block_ids = blocks.reshape(groups, -1)
    live_slots = (jnp.arange(K)[None, None, :] < counts[:, :, None]).reshape(groups, -1).astype(jnp.float32)
    catalog = advertiser_vectors.reshape(features, block_total, BLOCK)
    viewers = impression_vectors.reshape(features, groups, GROUP)
    extent = block_ids.shape[1] * BLOCK

    def allocate(prices, duals, group_no):
        chosen = block_ids[group_no]
        columns = jnp.take(catalog, chosen, axis=1).reshape(features, extent)
        viewer = lax.dynamic_index_in_dim(viewers, group_no, 1, keepdims=False)
        scores = jnp.dot(viewer.T, columns, preferred_element_type=jnp.float32)
        charged = jnp.take(prices.reshape(block_total, BLOCK), chosen, axis=0).reshape(extent)
        shadow = lax.dynamic_slice_in_dim(duals, group_no * GROUP, GROUP)
        eligible = jnp.repeat(live_slots[group_no], BLOCK)
        shares = jnp.clip(scores - charged[None, :] - shadow[:, None], 0.0, 1.0) * eligible[None, :]
        return shares, chosen, columns, viewer

    def totals(prices, duals):
        def advance(outlay, group_no):
            shares, chosen, _, _ = allocate(prices, duals, group_no)
            outlay = outlay.at[chosen].add(jnp.sum(shares, axis=0).reshape(-1, BLOCK))
            return outlay, jnp.sum(shares, axis=1)

        outlay, demand = lax.scan(advance, jnp.zeros((block_total, BLOCK), jnp.float32), jnp.arange(groups))
        return outlay.reshape(-1), demand.reshape(-1)

    prices = jnp.zeros((block_total * BLOCK,), jnp.float32)
    duals = jnp.zeros((groups * GROUP,), jnp.float32)
    for iteration in range(ITERS):
        outlay, demand = totals(prices, duals)
        prices = jnp.maximum(prices + outlay / spend_limits - 1.0, 0.0)
        duals = jnp.maximum(duals + demand / capacity - 1.0, 0.0)

    row_groups = groups // N_IMP

    def row_step(running, row_index):
        def group_step(partial_value, offset):
            shares, chosen, columns, viewer = allocate(prices, duals, row_index * row_groups + offset)
            weights = shares.astype(jnp.bfloat16)
            imp_cols = jnp.dot(columns, weights.T, preferred_element_type=jnp.float32)
            adv_terms = jnp.dot(viewer, weights, preferred_element_type=jnp.float32).reshape(features, -1, BLOCK)
            partial_value = partial_value.at[:, chosen].add(adv_terms)
            return partial_value, imp_cols

        partial_value, imp_cols = lax.scan(group_step, jnp.zeros((features, block_total, BLOCK), jnp.float32), jnp.arange(row_groups))
        rounded = lax.optimization_barrier((partial_value / GROUP).astype(jnp.bfloat16)).astype(jnp.float32)
        return running + rounded, imp_cols

    running, imp_cols = lax.scan(row_step, jnp.zeros((features, block_total, BLOCK), jnp.float32), jnp.arange(N_IMP))
    impression_grad = jnp.transpose(imp_cols, (2, 0, 1, 3)).reshape(features, -1).astype(jnp.bfloat16)
    advertiser_grad = running.reshape(features, -1).astype(jnp.bfloat16)
    return prices, duals, impression_grad, advertiser_grad
```

```python
import functools

import jax
import jax.numpy as jnp
from jax import lax
from jax.experimental import pallas as pl
from jax.experimental.pallas import tpu as pltpu
from jax.sharding import PartitionSpec as P


GROUP = 128
BLOCK = 128
PENALTY = 1e30

VMEM = pl.BlockSpec(memory_space=pltpu.VMEM)
SMEM = pl.BlockSpec(memory_space=pltpu.SMEM)
F32 = jnp.float32
BF16 = jnp.bfloat16
IMP = ("z", "x")
ADV = ("y", "core")
PARAMS = pltpu.CompilerParams(vmem_limit_bytes=16 << 20)


def slot_shares(group_no, slot, ids, counts, catalog, viewer, prices, shadow):
    first, second = ids[group_no, slot], ids[group_no, slot + 1]
    columns = jnp.concatenate([catalog[first], catalog[second]], axis=1)
    scores = jnp.dot(viewer, columns, preferred_element_type=F32)
    count = counts[group_no, 0]
    rows = []
    for place, block in ((slot, first), (slot + 1, second)):
        dead = jnp.where(place < count, 0.0, PENALTY).astype(F32)
        charged = dead if prices is None else prices[pl.ds(block, 1), :] + dead
        rows.append(jnp.broadcast_to(charged, (1, BLOCK)))
    scores = scores - jnp.concatenate(rows, axis=1)
    if shadow is not None:
        scores = scores - jnp.concatenate([shadow, shadow], axis=1)
    return jnp.clip(scores, 0.0, 1.0), columns, first, second


def column(row):
    return jnp.broadcast_to(row, (row.shape[1], row.shape[1])).T


def totals_kernel(first_pass, ids, counts, catalog, viewers_t, *refs):
    groups, slots = ids.shape
    if first_pass:
        outlay_out, demand_out, outlay_acc = refs
        prices = duals = None
    else:
        (outlays, old_prices, rate, duals,
         outlay_out, demand_out, prices, outlay_acc) = refs
        prices[...] = jnp.maximum(
            old_prices[...] + jnp.sum(outlays[...], axis=0) * rate[...] - 1.0, 0.0
        )
    outlay_acc[...] = jnp.zeros_like(outlay_acc)

    def step(group_no, _):
        start = pl.multiple_of(group_no * GROUP, GROUP)
        viewer = viewers_t[pl.ds(start, GROUP), :]
        shadow = None if first_pass else column(duals[pl.ds(group_no, 1), :])
        by_viewer = jnp.zeros((GROUP, BLOCK), F32)
        for slot in range(0, slots, 2):
            shares, _, first, second = slot_shares(
                group_no, slot, ids, counts, catalog, viewer, prices, shadow
            )
            by_viewer = by_viewer + (shares[:, :BLOCK] + shares[:, BLOCK:])
            folded = jnp.sum(shares.reshape(GROUP // 8, 8, 2 * BLOCK), axis=0)
            outlay_acc[first] += folded[:, :BLOCK]
            outlay_acc[second] += folded[:, BLOCK:]
        demand_out[pl.ds(group_no, 1), :] = jnp.sum(by_viewer.T, axis=0, keepdims=True)
        return 0

    lax.fori_loop(0, groups, step, 0)
    outlay = jnp.sum(outlay_acc[...], axis=1)
    for peer in range(outlay_out.shape[0]):
        outlay_out[peer] = outlay


def grads_kernel(
    ids, counts, catalog, viewers_t, viewers, outlays, old_prices, rate, duals,
    imp_out, adv_out, prices, adv_acc,
):
    groups, slots = ids.shape
    features = viewers.shape[0]
    prices[...] = jnp.maximum(
        old_prices[...] + jnp.sum(outlays[...], axis=0) * rate[...] - 1.0, 0.0
    )
    adv_acc[...] = jnp.zeros_like(adv_acc)

    def step(group_no, _):
        start = pl.multiple_of(group_no * GROUP, GROUP)
        viewer_t = viewers_t[pl.ds(start, GROUP), :]
        viewer = viewers[:, pl.ds(start, GROUP)]
        shadow = column(duals[pl.ds(group_no, 1), :])
        imp_part = jnp.zeros((features, GROUP), F32)
        for slot in range(0, slots, 2):
            shares, columns, first, second = slot_shares(
                group_no, slot, ids, counts, catalog, viewer_t, prices, shadow
            )
            weights = shares.astype(BF16)
            imp_part = imp_part + lax.dot_general(
                columns, weights, (((1,), (1,)), ((), ())), preferred_element_type=F32
            )
            adv_terms = jnp.dot(viewer, weights, preferred_element_type=F32)
            adv_acc[first] += adv_terms[:, :BLOCK]
            adv_acc[second] += adv_terms[:, BLOCK:]
        imp_out[group_no] = imp_part.astype(BF16)
        return 0

    lax.fori_loop(0, groups, step, 0)
    adv_out[...] = (adv_acc[...] * (1.0 / GROUP)).astype(BF16)


def spread(value, axis):
    copies = jnp.broadcast_to(value, (lax.axis_size(axis), *value.shape))
    return lax.all_to_all(copies, axis, 0, 0, tiled=True)


def to_all(value, axis):
    return lax.all_to_all(value, axis, 0, 0, tiled=True)


def local(impression_vectors, advertiser_vectors, spend_limits, capacity, blocks, counts):
    features = impression_vectors.shape[0]
    groups, _, slots = blocks.shape
    n_imp, n_adv = lax.axis_size(IMP), lax.axis_size(ADV)
    ids = blocks.reshape(groups, slots) // n_adv
    viewers_t = impression_vectors.T
    caps = capacity.reshape(groups, GROUP)
    catalog = spread(advertiser_vectors, IMP)
    spend = spread(spend_limits.reshape(1, BLOCK), IMP).reshape(n_imp, BLOCK)
    rate = 1.0 / spend

    exchange = (
        jax.ShapeDtypeStruct((n_imp, n_imp, BLOCK), F32),
        jax.ShapeDtypeStruct((groups, GROUP), F32),
    )
    priced = (jax.ShapeDtypeStruct((n_imp, BLOCK), F32),)
    scratch = [pltpu.VMEM((n_imp, 8, BLOCK), F32)]

    outlays, demand = pl.pallas_call(
        functools.partial(totals_kernel, True),
        in_specs=[SMEM, SMEM, VMEM, VMEM],
        out_specs=(VMEM, VMEM),
        out_shape=exchange,
        scratch_shapes=scratch,
        compiler_params=PARAMS,
    )(ids, counts, catalog, viewers_t)
    prices = jnp.zeros((n_imp, BLOCK), F32)
    duals = jnp.zeros((groups, GROUP), F32)

    def meet(outlays, demand, duals):
        outlays = to_all(outlays, IMP)
        pair = lax.all_gather(demand, "core", axis=0)
        demand = lax.psum((pair[0] + pair[1]).reshape(-1), "y").reshape(demand.shape)
        duals = jnp.maximum(duals + demand / caps - 1.0, 0.0)
        return outlays, duals

    for _ in range(2):
        outlays, duals = meet(outlays, demand, duals)
        outlays, demand, prices = pl.pallas_call(
            functools.partial(totals_kernel, False),
            in_specs=[SMEM, SMEM] + [VMEM] * 6,
            out_specs=(VMEM,) * 3,
            out_shape=exchange + priced,
            scratch_shapes=scratch,
            compiler_params=PARAMS,
        )(ids, counts, catalog, viewers_t, outlays, prices, rate, duals)
    outlays, duals = meet(outlays, demand, duals)
    imp_parts, adv_parts, prices = pl.pallas_call(
        grads_kernel,
        in_specs=[SMEM, SMEM] + [VMEM] * 7,
        out_specs=(VMEM,) * 3,
        out_shape=(
            jax.ShapeDtypeStruct((groups, features, GROUP), BF16),
            jax.ShapeDtypeStruct((n_imp, features, BLOCK), BF16),
        )
        + priced,
        scratch_shapes=[pltpu.VMEM((n_imp, features, BLOCK), F32)],
        compiler_params=PARAMS,
    )(ids, counts, catalog, viewers_t, impression_vectors, outlays, prices, rate, duals)
    adv_parts = to_all(adv_parts, IMP)
    imp_parts = to_all(imp_parts, ADV)
    impression_grad = jnp.sum(imp_parts.astype(F32), axis=0).astype(BF16)
    own_prices = lax.dynamic_index_in_dim(prices, lax.axis_index(IMP), 0, keepdims=False)
    advertiser_grad = jnp.sum(adv_parts.astype(F32), axis=0).astype(BF16)
    return own_prices, duals.reshape(-1), impression_grad, advertiser_grad


def solution(mesh):
    n_imp, n_adv = (mesh.shape[axis] for axis in ("imp", "adv"))
    chips = jax.sharding.Mesh(mesh.devices.reshape(n_imp // 4, 4, n_adv // 2, 2), IMP + ADV)
    return jax.shard_map(
        local,
        mesh=chips,
        in_specs=(
            P(None, IMP),
            P(None, IMP + ADV),
            P(IMP + ADV),
            P(IMP),
            P(IMP, ADV, None),
            P(IMP, ADV),
        ),
        out_specs=(P(IMP + ADV), P(IMP), P(None, IMP + ADV), P(None, IMP + ADV)),
        check_vma=False,
    )
```

```python
import functools

import jax
import jax.numpy as jnp
from jax import lax
from jax.experimental import pallas as pl
from jax.experimental.pallas import tpu as pltpu
from jax.sharding import PartitionSpec as P


GROUP = 128
BLOCK = 128
PARTS = 8
STRIP = 16
UNROLL = 2
DEAD = 1e30

F32 = jnp.float32
BF16 = jnp.bfloat16
IMP = ("z", "x")
ADV = ("y", "core")
VMEM = pl.BlockSpec(memory_space=pltpu.VMEM)
SMEM = pl.BlockSpec(memory_space=pltpu.SMEM)
PARAMS = pltpu.CompilerParams(vmem_limit_bytes=16 << 20)


def parts_of(value):
    high = value.astype(BF16).astype(F32)
    rest = value - high
    middle = rest.astype(BF16).astype(F32)
    return high, middle, rest - middle


def rows_of(rows, count):
    place = lax.broadcasted_iota(jnp.int32, (count, rows[0].shape[1]), 0)
    stacked = jnp.zeros((count, rows[0].shape[1]), F32)
    for index, row in enumerate(rows):
        stacked = jnp.where(place == index, row, stacked)
    return stacked


def pack_kernel(vectors, spend, out):
    features = vectors.shape[0]
    columns = vectors[...]
    limits = rows_of(parts_of(spend[...]), PARTS).astype(BF16)
    for peer in range(out.shape[0]):
        out[peer, :features, :] = columns
        out[peer, features:, :] = limits


def new_prices(outlays, old_prices, rate):
    return jnp.maximum(old_prices[...] + jnp.sum(outlays[...], axis=0) * rate[...] - 1.0, 0.0)


def set_strips(strips, prices):
    blocks = strips.shape[0] - 1
    strips[...] = jnp.zeros_like(strips)
    dead = jnp.full((1, BLOCK), -DEAD, F32)
    strips[blocks, :, :] = rows_of([dead], STRIP).astype(BF16)
    if prices is not None:
        parts = parts_of(-prices)
        for block in range(blocks):
            rows = rows_of([part[block : block + 1, :] for part in parts], 8)
            rows = jnp.concatenate([rows, jnp.zeros((STRIP - 8, BLOCK), F32)], axis=0)
            strips[block, :, :] = rows.astype(BF16)


def turned_duals(duals, width):
    parts = parts_of(duals)
    above = jnp.zeros((width - 3 * duals.shape[0], GROUP), F32)
    return jnp.concatenate([above, *parts], axis=0).T.astype(BF16)


def pair_shares(group_no, slot, ids, catalog, strips, viewer, groups, duals):
    features = catalog.shape[1] - PARTS
    last = catalog.shape[0] - 1
    first, second = ids[group_no, slot], ids[group_no, slot + 1]
    vectors = jnp.concatenate(
        [
            catalog[jnp.minimum(first, last), :features, :],
            catalog[jnp.minimum(second, last), :features, :],
        ],
        axis=1,
    )
    rows = [vectors, jnp.concatenate([strips[first], strips[second]], axis=1)]
    if duals:
        place = lax.broadcasted_iota(jnp.int32, (groups, 2 * BLOCK), 0)
        rows += [jnp.where(place == group_no, -1.0, 0.0).astype(BF16)] * 3
    scores = jnp.dot(viewer, jnp.concatenate(rows, axis=0), preferred_element_type=F32)
    return jnp.clip(scores, 0.0, 1.0), vectors, first, second


def totals_kernel(first_pass, ids, catalog, viewers_t, *refs):
    groups, slots = ids.shape
    features = catalog.shape[1] - PARTS
    if first_pass:
        outlay_out, demand_out, rate, strips, outlay_acc, demand_acc = refs
        limits = catalog[:, features:, :].astype(F32)
        rate[...] = 1.0 / jnp.sum(limits, axis=1)
        set_strips(strips, None)
    else:
        (outlays, old_prices, rate, duals,
         outlay_out, demand_out, prices, strips, outlay_acc, demand_acc) = refs
        prices[...] = new_prices(outlays, old_prices, rate)
        set_strips(strips, prices[...])
        turned = turned_duals(duals[...], viewers_t.shape[1])
    outlay_acc[...] = jnp.zeros_like(outlay_acc)
    demand_acc[...] = jnp.zeros_like(demand_acc)
    lane = lax.broadcasted_iota(jnp.int32, (GROUP, BLOCK), 1)

    def step(group_no, _):
        start = pl.multiple_of(group_no * GROUP, GROUP)
        viewer = viewers_t[pl.ds(start, GROUP), :]
        viewer = viewer[:, : features + STRIP] if first_pass else viewer + turned
        by_viewer = jnp.zeros((GROUP, BLOCK), F32)
        for slot in range(0, slots, 2):
            shares, _, first, second = pair_shares(
                group_no, slot, ids, catalog, strips, viewer, groups, not first_pass
            )
            by_viewer = by_viewer + (shares[:, :BLOCK] + shares[:, BLOCK:])
            folded = jnp.sum(shares.reshape(GROUP // 8, 8, 2 * BLOCK), axis=0)
            outlay_acc[first] += folded[:, :BLOCK]
            outlay_acc[second] += folded[:, BLOCK:]
        demand = jnp.sum(by_viewer, axis=1, keepdims=True)
        demand_acc[...] = jnp.where(lane == group_no, demand, demand_acc[...])
        return 0

    lax.fori_loop(0, groups, step, 0, unroll=UNROLL)
    demand_out[...] = demand_acc[...].T[:groups, :]
    peers = outlay_out.shape[0]
    outlay = jnp.sum(outlay_acc[:peers], axis=1)
    for peer in range(peers):
        outlay_out[peer] = outlay


def adv_kernel(
    ids, own, catalog, viewers_t, viewers, outlays, old_prices, rate, duals,
    adv_out, own_prices, duals_out, strips_out, adv_acc, prices,
):
    groups, slots = ids.shape
    prices[...] = new_prices(outlays, old_prices, rate)
    own_prices[...] = prices[pl.ds(own[0], 1), :]
    duals_out[...] = duals[...]
    set_strips(strips_out, prices[...])
    turned = turned_duals(duals[...], viewers_t.shape[1])
    adv_acc[...] = jnp.zeros_like(adv_acc)

    def step(group_no, _):
        start = pl.multiple_of(group_no * GROUP, GROUP)
        viewer_t = viewers_t[pl.ds(start, GROUP), :] + turned
        viewer = viewers[:, pl.ds(start, GROUP)]
        for slot in range(0, slots, 2):
            shares, _, first, second = pair_shares(
                group_no, slot, ids, catalog, strips_out, viewer_t, groups, True
            )
            terms = jnp.dot(viewer, shares.astype(BF16), preferred_element_type=F32)
            adv_acc[first] += terms[:, :BLOCK]
            adv_acc[second] += terms[:, BLOCK:]
        return 0

    lax.fori_loop(0, groups, step, 0, unroll=UNROLL)
    adv_out[...] = (adv_acc[: adv_out.shape[0]] * (1.0 / GROUP)).astype(BF16)


def imp_kernel(ids, catalog, viewers_t, strips, duals, imp_out):
    groups, slots = ids.shape
    features = catalog.shape[1] - PARTS
    turned = turned_duals(duals[...], viewers_t.shape[1])

    def step(group_no, _):
        start = pl.multiple_of(group_no * GROUP, GROUP)
        viewer_t = viewers_t[pl.ds(start, GROUP), :] + turned
        imp_part = jnp.zeros((features, GROUP), F32)
        for slot in range(0, slots, 2):
            shares, vectors, _, _ = pair_shares(
                group_no, slot, ids, catalog, strips, viewer_t, groups, True
            )
            imp_part = imp_part + lax.dot_general(
                vectors, shares.astype(BF16), (((1,), (1,)), ((), ())),
                preferred_element_type=F32,
            )
        imp_out[lax.rem(group_no, 2), lax.div(group_no, 2)] = imp_part.astype(BF16)
        return 0

    lax.fori_loop(0, groups, step, 0, unroll=UNROLL)


def to_all(value, axis):
    return lax.all_to_all(value, axis, 0, 0, tiled=True)


def call(kernel, n_smem, out_shape, scratch, *args):
    return pl.pallas_call(
        kernel,
        in_specs=[SMEM] * n_smem + [VMEM] * (len(args) - n_smem),
        out_specs=(VMEM,) * len(out_shape),
        out_shape=tuple(jax.ShapeDtypeStruct(shape, dtype) for shape, dtype in out_shape),
        scratch_shapes=[pltpu.VMEM(shape, dtype) for shape, dtype in scratch],
        compiler_params=PARAMS,
    )(*args)


def local(impression_vectors, advertiser_vectors, spend_limits, capacity, blocks, counts):
    features = impression_vectors.shape[0]
    groups, _, slots = blocks.shape
    n_imp, n_adv = lax.axis_size(IMP), lax.axis_size(ADV)
    live = jnp.arange(slots)[None, :] < counts
    ids = jnp.where(live, blocks.reshape(groups, slots) // n_adv, n_imp)
    own = lax.axis_index(IMP).astype(jnp.int32).reshape(1)
    caps = capacity.reshape(groups, GROUP)
    ones = jnp.ones((3, impression_vectors.shape[1]), BF16)
    rest = STRIP - 3 + 3 * groups
    zeros = jnp.zeros((rest, impression_vectors.shape[1]), BF16)
    viewers_t = jnp.concatenate([impression_vectors, ones, zeros], axis=0).T

    (packed,) = call(
        pack_kernel, 0, [((n_imp, features + PARTS, BLOCK), BF16)], [],
        advertiser_vectors, spend_limits.reshape(1, BLOCK),
    )
    catalog = to_all(packed, IMP)

    exchange = [((n_imp, n_imp, BLOCK), F32), ((groups, GROUP), F32)]
    levels = [((n_imp, BLOCK), F32)]
    strips = [((n_imp + 1, STRIP, BLOCK), BF16)]
    sums = [((n_imp + 1, 8, BLOCK), F32), ((GROUP, BLOCK), F32)]

    outlays, demand, rate = call(
        functools.partial(totals_kernel, True), 1, exchange + levels, strips + sums,
        ids, catalog, viewers_t,
    )
    prices = jnp.zeros((n_imp, BLOCK), F32)
    duals = jnp.zeros((groups, GROUP), F32)

    def meet(outlays, demand, duals):
        outlays = to_all(outlays, IMP)
        pair = lax.all_gather(demand, "core", axis=0)
        demand = lax.psum((pair[0] + pair[1]).reshape(-1), "y").reshape(demand.shape)
        duals = jnp.maximum(duals + demand / caps - 1.0, 0.0)
        return outlays, duals

    for _ in range(2):
        outlays, duals = meet(outlays, demand, duals)
        outlays, demand, prices = call(
            functools.partial(totals_kernel, False), 1, exchange + levels,
            strips + sums,
            ids, catalog, viewers_t, outlays, prices, rate, duals,
        )
    outlays, duals = meet(outlays, demand, duals)
    adv_parts, own_prices, out_duals, strip_rows = call(
        adv_kernel, 2,
        [
            ((n_imp, features, BLOCK), BF16),
            ((1, BLOCK), F32),
            ((groups, GROUP), F32),
            *strips,
        ],
        [((n_imp + 1, features, BLOCK), F32)] + levels,
        ids, own, catalog, viewers_t, impression_vectors, outlays, prices, rate, duals,
    )
    adv_parts = to_all(adv_parts, IMP)
    (imp_parts,) = call(
        imp_kernel, 1, [((2, groups // 2, features, GROUP), BF16)], [],
        ids, catalog, viewers_t, strip_rows, duals,
    )
    core = lax.axis_index("core")
    kept = lax.dynamic_index_in_dim(imp_parts, core, 0, keepdims=False)
    given = lax.dynamic_index_in_dim(imp_parts, 1 - core, 0, keepdims=False)
    given = lax.ppermute(given, "core", [(0, 1), (1, 0)])
    imp_parts = (kept.astype(F32) + given.astype(F32)).astype(BF16)
    imp_parts = to_all(imp_parts, "y")
    impression_grad = jnp.sum(imp_parts.astype(F32), axis=0).astype(BF16)
    advertiser_grad = jnp.sum(adv_parts.astype(F32), axis=0).astype(BF16)
    return own_prices.reshape(-1), out_duals.reshape(-1), impression_grad, advertiser_grad


def solution(mesh):
    n_imp, n_adv = (mesh.shape[axis] for axis in ("imp", "adv"))
    chips = jax.sharding.Mesh(mesh.devices.reshape(n_imp // 4, 4, n_adv // 2, 2), IMP + ADV)
    return jax.shard_map(
        local,
        mesh=chips,
        in_specs=(
            P(None, IMP),
            P(None, IMP + ADV),
            P(IMP + ADV),
            P(IMP),
            P(IMP, ADV, None),
            P(IMP, ADV),
        ),
        out_specs=(P(IMP + ADV), P(IMP), P(None, IMP + ADV), P(None, IMP + ADV)),
        check_vma=False,
    )
```

```python
import functools

import jax
import jax.numpy as jnp
from jax import lax
from jax.experimental import pallas as pl
from jax.experimental.pallas import tpu as pltpu
from jax.sharding import PartitionSpec as P


GROUP = 128
BLOCK = 128
PARTS = 8
STRIP = 16
UNROLL = 24
DEAD = 1e30

F32 = jnp.float32
BF16 = jnp.bfloat16
IMP = ("z", "x")
ADV = ("y", "core")
VMEM = pl.BlockSpec(memory_space=pltpu.VMEM)
SMEM = pl.BlockSpec(memory_space=pltpu.SMEM)
PARAMS = pltpu.CompilerParams(vmem_limit_bytes=16 << 20)


def parts_of(value):
    high = value.astype(BF16).astype(F32)
    rest = value - high
    middle = rest.astype(BF16).astype(F32)
    return high, middle, rest - middle


def rows_of(rows, count):
    place = lax.broadcasted_iota(jnp.int32, (count, rows[0].shape[1]), 0)
    stacked = jnp.zeros((count, rows[0].shape[1]), F32)
    for index, row in enumerate(rows):
        stacked = jnp.where(place == index, row, stacked)
    return stacked


def pack_kernel(vectors, spend, out):
    features = vectors.shape[0]
    columns = vectors[...]
    limits = rows_of(parts_of(spend[...]), PARTS).astype(BF16)
    for peer in range(out.shape[0]):
        out[peer, :features, :] = columns
        out[peer, features:, :] = limits


def new_prices(outlays, old_prices, rate):
    return jnp.maximum(old_prices[...] + jnp.sum(outlays[...], axis=0) * rate[...] - 1.0, 0.0)


def set_strips(strips, prices):
    blocks = strips.shape[0] - 1
    strips[...] = jnp.zeros_like(strips)
    dead = jnp.full((1, BLOCK), -DEAD, F32)
    strips[blocks, :, :] = rows_of([dead], STRIP).astype(BF16)
    if prices is not None:
        parts = parts_of(-prices)
        for block in range(blocks):
            rows = rows_of([part[block : block + 1, :] for part in parts], 8)
            rows = jnp.concatenate([rows, jnp.zeros((STRIP - 8, BLOCK), F32)], axis=0)
            strips[block, :, :] = rows.astype(BF16)


def turned_duals(duals, width):
    parts = parts_of(duals)
    above = jnp.zeros((width - 3 * duals.shape[0], GROUP), F32)
    return jnp.concatenate([above, *parts], axis=0).T.astype(BF16)


def pair_scores(index, work, catalog, strips, viewers_t, turned):
    features = catalog.shape[1] - PARTS
    last = catalog.shape[0] - 1
    group_no, first, second = (work[row, index] for row in range(3))
    viewer = viewers_t[pl.ds(pl.multiple_of(group_no * GROUP, GROUP), GROUP), :]
    vectors = jnp.concatenate(
        [
            catalog[jnp.minimum(first, last), :features, :],
            catalog[jnp.minimum(second, last), :features, :],
        ],
        axis=1,
    )
    rows = [vectors, jnp.concatenate([strips[first], strips[second]], axis=1)]
    if turned is None:
        viewer = viewer[:, : features + STRIP]
    else:
        viewer = viewer + turned
        groups = (viewers_t.shape[1] - features - STRIP) // 3
        place = lax.broadcasted_iota(jnp.int32, (groups, 2 * BLOCK), 0)
        rows += [jnp.where(place == group_no, -1.0, 0.0).astype(BF16)] * 3
    scores = jnp.dot(viewer, jnp.concatenate(rows, axis=0), preferred_element_type=F32)
    return scores, vectors, group_no, first, second


def for_pairs(work, unroll, body):
    def step(number, _):
        body([number * unroll + offset for offset in range(unroll)])
        return 0

    lax.fori_loop(0, lax.div(work[3, 0] + (unroll - 1), unroll), step, 0)


def totals_kernel(first_pass, work, catalog, viewers_t, *refs):
    features = catalog.shape[1] - PARTS
    turned = None
    if first_pass:
        outlay_out, demand_out, rate, strips, outlay_acc, demand_acc = refs
        limits = catalog[:, features:, :].astype(F32)
        rate[...] = 1.0 / jnp.sum(limits, axis=1)
        set_strips(strips, None)
    else:
        (outlays, old_prices, rate, duals,
         outlay_out, demand_out, prices, strips, outlay_acc, demand_acc) = refs
        prices[...] = new_prices(outlays, old_prices, rate)
        set_strips(strips, prices[...])
        turned = turned_duals(duals[...], viewers_t.shape[1])
    outlay_acc[...] = jnp.zeros_like(outlay_acc)
    demand_acc[...] = jnp.zeros_like(demand_acc)

    lane = lax.broadcasted_iota(jnp.int32, (GROUP, 128), 1)

    def pairs(indices):
        demand = demand_acc[...]
        scored = [pair_scores(i, work, catalog, strips, viewers_t, turned) for i in indices]
        for scores, _, group_no, first, second in scored:
            shares = jnp.clip(scores, 0.0, 1.0)
            total = jnp.sum(shares[:, :BLOCK] + shares[:, BLOCK:], axis=1, keepdims=True)
            demand = demand + jnp.where(lane == group_no, total, 0.0)
            folded = jnp.sum(shares.reshape(GROUP // 8, 8, 2 * BLOCK), axis=0)
            outlay_acc[first] += folded[:, :BLOCK]
            outlay_acc[second] += folded[:, BLOCK:]
        demand_acc[...] = demand

    for_pairs(work, UNROLL, pairs)
    demand_out[...] = demand_acc[...].T[: demand_out.shape[0], :]
    peers = outlay_out.shape[0]
    outlay = jnp.sum(outlay_acc[:peers], axis=1)
    for peer in range(peers):
        outlay_out[peer] = outlay


def adv_kernel(
    work, own, catalog, viewers_t, viewers, outlays, old_prices, rate, duals,
    adv_out, own_prices, duals_out, strips_out, adv_acc, prices,
):
    prices[...] = new_prices(outlays, old_prices, rate)
    own_prices[...] = prices[pl.ds(own[0], 1), :]
    duals_out[...] = duals[...]
    set_strips(strips_out, prices[...])
    turned = turned_duals(duals[...], viewers_t.shape[1])
    adv_acc[...] = jnp.zeros_like(adv_acc)

    def pairs(indices):
        scored = [pair_scores(i, work, catalog, strips_out, viewers_t, turned) for i in indices]
        weighed = [jnp.clip(one[0], 0.0, 1.0).astype(BF16) for one in scored]
        for weights, (_, _, group_no, first, second) in zip(weighed, scored):
            viewer = viewers[:, pl.ds(pl.multiple_of(group_no * GROUP, GROUP), GROUP)]
            terms = jnp.dot(viewer, weights, preferred_element_type=F32)
            adv_acc[first] += terms[:, :BLOCK]
            adv_acc[second] += terms[:, BLOCK:]

    for_pairs(work, UNROLL, pairs)
    adv_out[...] = (adv_acc[: adv_out.shape[0]] * (1.0 / GROUP)).astype(BF16)


def imp_kernel(work, catalog, viewers_t, strips, duals, imp_out, imp_acc):
    turned = turned_duals(duals[...], viewers_t.shape[1])
    imp_acc[...] = jnp.zeros_like(imp_acc)

    def pairs(indices):
        scored = [pair_scores(i, work, catalog, strips, viewers_t, turned) for i in indices]
        weighed = [jnp.clip(one[0], 0.0, 1.0).astype(BF16) for one in scored]
        for weights, (_, vectors, group_no, _, _) in zip(weighed, scored):
            imp_acc[group_no] += lax.dot_general(
                vectors, weights, (((1,), (1,)), ((), ())), preferred_element_type=F32
            )

    for_pairs(work, UNROLL, pairs)
    for group_no in range(imp_acc.shape[0]):
        imp_out[group_no % 2, group_no // 2] = imp_acc[group_no].astype(BF16)


def to_all(value, axis):
    return lax.all_to_all(value, axis, 0, 0, tiled=True)


def work_list(ids, counts, dead):
    _, slots = ids.shape
    ids = jnp.where(jnp.arange(slots)[None, :] < counts, ids, dead)
    live = (jnp.arange(0, slots, 2)[None, :] < counts).reshape(-1)
    pairs = jnp.arange(live.size)
    entries = jnp.arange(-(-live.size // UNROLL) * UNROLL)
    place = jnp.sum(live[None, :] & (pairs[None, :] < pairs[:, None]), axis=1)
    chosen = live[None, :] & (place[None, :] == entries[:, None])
    group_no = pairs // (slots // 2)
    rows = [
        jnp.sum(jnp.where(chosen, row[None, :] - rest, 0), axis=1) + rest
        for row, rest in ((group_no, 0), (ids[:, ::2].reshape(-1), dead), (ids[:, 1::2].reshape(-1), dead))
    ]
    rows.append(jnp.full_like(entries, jnp.sum(live)))
    return jnp.stack(rows).astype(jnp.int32)


def call(kernel, n_smem, out_shape, scratch, *args):
    return pl.pallas_call(
        kernel,
        in_specs=[SMEM] * n_smem + [VMEM] * (len(args) - n_smem),
        out_specs=(VMEM,) * len(out_shape),
        out_shape=tuple(jax.ShapeDtypeStruct(shape, dtype) for shape, dtype in out_shape),
        scratch_shapes=[pltpu.VMEM(shape, dtype) for shape, dtype in scratch],
        compiler_params=PARAMS,
    )(*args)


def local(impression_vectors, advertiser_vectors, spend_limits, capacity, blocks, counts):
    features = impression_vectors.shape[0]
    groups, _, slots = blocks.shape
    n_imp, n_adv = lax.axis_size(IMP), lax.axis_size(ADV)
    work = work_list(blocks.reshape(groups, slots) // n_adv, counts, n_imp)
    own = lax.axis_index(IMP).astype(jnp.int32).reshape(1)
    caps = capacity.reshape(groups, GROUP)
    ones = jnp.ones((3, impression_vectors.shape[1]), BF16)
    rest = STRIP - 3 + 3 * groups
    zeros = jnp.zeros((rest, impression_vectors.shape[1]), BF16)
    viewers_t = jnp.concatenate([impression_vectors, ones, zeros], axis=0).T

    (packed,) = call(
        pack_kernel, 0, [((n_imp, features + PARTS, BLOCK), BF16)], [],
        advertiser_vectors, spend_limits.reshape(1, BLOCK),
    )
    catalog = to_all(packed, IMP)

    exchange = [((n_imp, n_imp, BLOCK), F32), ((groups, GROUP), F32)]
    levels = [((n_imp, BLOCK), F32)]
    strips = [((n_imp + 1, STRIP, BLOCK), BF16)]
    sums = [((n_imp + 1, 8, BLOCK), F32), ((GROUP, 128), F32)]

    outlays, demand, rate = call(
        functools.partial(totals_kernel, True), 1, exchange + levels, strips + sums,
        work, catalog, viewers_t,
    )
    prices = jnp.zeros((n_imp, BLOCK), F32)
    duals = jnp.zeros((groups, GROUP), F32)

    def meet(outlays, demand, duals):
        outlays = to_all(outlays, IMP)
        pair = lax.all_gather(demand, "core", axis=0)
        demand = lax.psum((pair[0] + pair[1]).reshape(-1), "y").reshape(demand.shape)
        duals = jnp.maximum(duals + demand / caps - 1.0, 0.0)
        return outlays, duals

    for _ in range(2):
        outlays, duals = meet(outlays, demand, duals)
        outlays, demand, prices = call(
            functools.partial(totals_kernel, False), 1, exchange + levels,
            strips + sums,
            work, catalog, viewers_t, outlays, prices, rate, duals,
        )
    outlays, duals = meet(outlays, demand, duals)
    adv_parts, own_prices, out_duals, strip_rows = call(
        adv_kernel, 2,
        [
            ((n_imp, features, BLOCK), BF16),
            ((1, BLOCK), F32),
            ((groups, GROUP), F32),
            *strips,
        ],
        [((n_imp + 1, features, BLOCK), F32)] + levels,
        work, own, catalog, viewers_t, impression_vectors, outlays, prices, rate, duals,
    )
    adv_parts = to_all(adv_parts, IMP)
    (imp_parts,) = call(
        imp_kernel, 1, [((2, groups // 2, features, GROUP), BF16)],
        [((groups, features, GROUP), F32)],
        work, catalog, viewers_t, strip_rows, duals,
    )
    core = lax.axis_index("core")
    kept = lax.dynamic_index_in_dim(imp_parts, core, 0, keepdims=False)
    given = lax.dynamic_index_in_dim(imp_parts, 1 - core, 0, keepdims=False)
    given = lax.ppermute(given, "core", [(0, 1), (1, 0)])
    imp_parts = (kept.astype(F32) + given.astype(F32)).astype(BF16)
    imp_parts = to_all(imp_parts, "y")
    impression_grad = jnp.sum(imp_parts.astype(F32), axis=0).astype(BF16)
    advertiser_grad = jnp.sum(adv_parts.astype(F32), axis=0).astype(BF16)
    return own_prices.reshape(-1), out_duals.reshape(-1), impression_grad, advertiser_grad


def solution(mesh):
    n_imp, n_adv = (mesh.shape[axis] for axis in ("imp", "adv"))
    chips = jax.sharding.Mesh(mesh.devices.reshape(n_imp // 4, 4, n_adv // 2, 2), IMP + ADV)
    return jax.shard_map(
        local,
        mesh=chips,
        in_specs=(
            P(None, IMP),
            P(None, IMP + ADV),
            P(IMP + ADV),
            P(IMP),
            P(IMP, ADV, None),
            P(IMP, ADV),
        ),
        out_specs=(P(IMP + ADV), P(IMP), P(None, IMP + ADV), P(None, IMP + ADV)),
        check_vma=False,
    )
```

```python
import functools

import jax
import jax.numpy as jnp
from jax import lax
from jax.experimental import pallas as pl
from jax.experimental.pallas import tpu as pltpu
from jax.sharding import PartitionSpec as P


GROUP = 128
BLOCK = 128
PARTS = 8
STRIP = 16
UNROLL = 24
DEAD = 1e30

F32 = jnp.float32
BF16 = jnp.bfloat16
IMP = ("z", "x")
ADV = "adv"
VMEM = pl.BlockSpec(memory_space=pltpu.VMEM)
SMEM = pl.BlockSpec(memory_space=pltpu.SMEM)
PARAMS = pltpu.CompilerParams(vmem_limit_bytes=16 << 20)


def parts_of(value):
    high = value.astype(BF16).astype(F32)
    rest = value - high
    middle = rest.astype(BF16).astype(F32)
    return high, middle, rest - middle


def rows_of(rows, count):
    place = lax.broadcasted_iota(jnp.int32, (count, rows[0].shape[1]), 0)
    stacked = jnp.zeros((count, rows[0].shape[1]), F32)
    for index, row in enumerate(rows):
        stacked = jnp.where(place == index, row, stacked)
    return stacked


def pack_kernel(vectors, spend, out):
    features = vectors.shape[0]
    columns = vectors[...]
    limits = rows_of(parts_of(spend[...]), PARTS).astype(BF16)
    for peer in range(out.shape[0]):
        out[peer, :features, :] = columns
        out[peer, features:, :] = limits


def new_prices(outlays, old_prices, rate):
    return jnp.maximum(old_prices[...] + jnp.sum(outlays[...], axis=0) * rate[...] - 1.0, 0.0)


def set_strips(strips, prices):
    blocks = strips.shape[0] - 1
    strips[...] = jnp.zeros_like(strips)
    dead = jnp.full((1, BLOCK), -DEAD, F32)
    strips[blocks, :, :] = rows_of([dead], STRIP).astype(BF16)
    if prices is not None:
        parts = parts_of(-prices)
        for block in range(blocks):
            rows = rows_of([part[block : block + 1, :] for part in parts], 8)
            rows = jnp.concatenate([rows, jnp.zeros((STRIP - 8, BLOCK), F32)], axis=0)
            strips[block, :, :] = rows.astype(BF16)


def turned_duals(duals, width):
    parts = parts_of(duals)
    above = jnp.zeros((width - 3 * duals.shape[0], GROUP), F32)
    return jnp.concatenate([above, *parts], axis=0).T.astype(BF16)


def pair_scores(index, work, catalog, strips, viewers_t, turned):
    features = catalog.shape[1] - PARTS
    last = catalog.shape[0] - 1
    group_no, first, second = (work[row, index] for row in range(3))
    viewer = viewers_t[pl.ds(pl.multiple_of(group_no * GROUP, GROUP), GROUP), :]
    vectors = jnp.concatenate(
        [
            catalog[jnp.minimum(first, last), :features, :],
            catalog[jnp.minimum(second, last), :features, :],
        ],
        axis=1,
    )
    rows = [vectors, jnp.concatenate([strips[first], strips[second]], axis=1)]
    if turned is None:
        viewer = viewer[:, : features + STRIP]
    else:
        viewer = viewer + turned
        groups = (viewers_t.shape[1] - features - STRIP) // 3
        place = lax.broadcasted_iota(jnp.int32, (groups, 2 * BLOCK), 0)
        rows += [jnp.where(place == group_no, -1.0, 0.0).astype(BF16)] * 3
    scores = jnp.dot(viewer, jnp.concatenate(rows, axis=0), preferred_element_type=F32)
    return scores, vectors, group_no, first, second


def for_pairs(work, unroll, body):
    def step(number, _):
        body([number * unroll + offset for offset in range(unroll)])
        return 0

    lax.fori_loop(0, lax.div(work[3, 0] + (unroll - 1), unroll), step, 0)


def totals_kernel(first_pass, work, catalog, viewers_t, *refs):
    features = catalog.shape[1] - PARTS
    turned = None
    if first_pass:
        outlay_out, demand_out, rate, strips, outlay_acc, demand_acc = refs
        limits = catalog[:, features:, :].astype(F32)
        rate[...] = 1.0 / jnp.sum(limits, axis=1)
        set_strips(strips, None)
    else:
        (outlays, old_prices, rate, duals,
         outlay_out, demand_out, prices, strips, outlay_acc, demand_acc) = refs
        prices[...] = new_prices(outlays, old_prices, rate)
        set_strips(strips, prices[...])
        turned = turned_duals(duals[...], viewers_t.shape[1])
    outlay_acc[...] = jnp.zeros_like(outlay_acc)
    demand_acc[...] = jnp.zeros_like(demand_acc)

    lane = lax.broadcasted_iota(jnp.int32, (GROUP, 128), 1)

    def pairs(indices):
        demand = demand_acc[...]
        scored = [pair_scores(i, work, catalog, strips, viewers_t, turned) for i in indices]
        for scores, _, group_no, first, second in scored:
            shares = jnp.clip(scores, 0.0, 1.0)
            total = jnp.sum(shares[:, :BLOCK] + shares[:, BLOCK:], axis=1, keepdims=True)
            demand = demand + jnp.where(lane == group_no, total, 0.0)
            folded = jnp.sum(shares.reshape(GROUP // 8, 8, 2 * BLOCK), axis=0)
            outlay_acc[first] += folded[:, :BLOCK]
            outlay_acc[second] += folded[:, BLOCK:]
        demand_acc[...] = demand

    for_pairs(work, UNROLL, pairs)
    demand_out[...] = demand_acc[...].T[: demand_out.shape[0], :]
    peers = outlay_out.shape[0]
    outlay = jnp.sum(outlay_acc[:peers], axis=1)
    for peer in range(peers):
        outlay_out[peer] = outlay


def adv_kernel(
    work, own, catalog, viewers_t, viewers, outlays, old_prices, rate, duals,
    adv_out, own_prices, duals_out, strips_out, adv_acc, prices,
):
    prices[...] = new_prices(outlays, old_prices, rate)
    own_prices[...] = prices[pl.ds(own[0], 1), :]
    duals_out[...] = duals[...]
    set_strips(strips_out, prices[...])
    turned = turned_duals(duals[...], viewers_t.shape[1])
    adv_acc[...] = jnp.zeros_like(adv_acc)

    def pairs(indices):
        scored = [pair_scores(i, work, catalog, strips_out, viewers_t, turned) for i in indices]
        weighed = [jnp.clip(one[0], 0.0, 1.0).astype(BF16) for one in scored]
        for weights, (_, _, group_no, first, second) in zip(weighed, scored):
            viewer = viewers[:, pl.ds(pl.multiple_of(group_no * GROUP, GROUP), GROUP)]
            terms = jnp.dot(viewer, weights, preferred_element_type=F32)
            adv_acc[first] += terms[:, :BLOCK]
            adv_acc[second] += terms[:, BLOCK:]

    for_pairs(work, UNROLL, pairs)
    adv_out[...] = (adv_acc[: adv_out.shape[0]] * (1.0 / GROUP)).astype(BF16)


def imp_kernel(work, catalog, viewers_t, strips, duals, imp_out, imp_acc):
    turned = turned_duals(duals[...], viewers_t.shape[1])
    imp_acc[...] = jnp.zeros_like(imp_acc)

    def pairs(indices):
        scored = [pair_scores(i, work, catalog, strips, viewers_t, turned) for i in indices]
        weighed = [jnp.clip(one[0], 0.0, 1.0).astype(BF16) for one in scored]
        for weights, (_, vectors, group_no, _, _) in zip(weighed, scored):
            imp_acc[group_no] += lax.dot_general(
                vectors, weights, (((1,), (1,)), ((), ())), preferred_element_type=F32
            )

    for_pairs(work, UNROLL, pairs)
    for group_no in range(imp_acc.shape[0]):
        imp_out[ring_of(group_no), group_no // 2] = imp_acc[group_no]


def chip_groups():
    return [[a, a + 1] for a in range(0, lax.axis_size(ADV), 2)]


def ring_of(place):
    return (place // 2 + place + 1) % 2


def ring_groups():
    places = range(lax.axis_size(ADV))
    return [[place for place in places if ring_of(place) == ring] for ring in (0, 1)]


def to_all(value, axis):
    return lax.all_to_all(value, axis, 0, 0, tiled=True)


def work_list(ids, counts, dead):
    _, slots = ids.shape
    ids = jnp.where(jnp.arange(slots)[None, :] < counts, ids, dead)
    live = (jnp.arange(0, slots, 2)[None, :] < counts).reshape(-1)
    pairs = jnp.arange(live.size)
    entries = jnp.arange(-(-live.size // UNROLL) * UNROLL)
    place = jnp.sum(live[None, :] & (pairs[None, :] < pairs[:, None]), axis=1)
    chosen = live[None, :] & (place[None, :] == entries[:, None])
    group_no = pairs // (slots // 2)
    rows = [
        jnp.sum(jnp.where(chosen, row[None, :] - rest, 0), axis=1) + rest
        for row, rest in ((group_no, 0), (ids[:, ::2].reshape(-1), dead), (ids[:, 1::2].reshape(-1), dead))
    ]
    rows.append(jnp.full_like(entries, jnp.sum(live)))
    return jnp.stack(rows).astype(jnp.int32)


def call(kernel, n_smem, out_shape, scratch, *args, params=PARAMS):
    return pl.pallas_call(
        kernel,
        in_specs=[SMEM] * n_smem + [VMEM] * (len(args) - n_smem),
        out_specs=(VMEM,) * len(out_shape),
        out_shape=tuple(jax.ShapeDtypeStruct(shape, dtype) for shape, dtype in out_shape),
        scratch_shapes=[pltpu.VMEM(shape, dtype) for shape, dtype in scratch],
        compiler_params=params,
    )(*args)


def local(impression_vectors, advertiser_vectors, spend_limits, capacity, blocks, counts):
    features = impression_vectors.shape[0]
    groups, _, slots = blocks.shape
    n_imp, n_adv = lax.axis_size(IMP), lax.axis_size(ADV)
    work = work_list(blocks.reshape(groups, slots) // n_adv, counts, n_imp)
    own = lax.axis_index(IMP).astype(jnp.int32).reshape(1)
    caps = capacity.reshape(groups, GROUP)
    ones = jnp.ones((3, impression_vectors.shape[1]), BF16)
    rest = STRIP - 3 + 3 * groups
    zeros = jnp.zeros((rest, impression_vectors.shape[1]), BF16)
    viewers_t = jnp.concatenate([impression_vectors, ones, zeros], axis=0).T

    (packed,) = call(
        pack_kernel, 0, [((n_imp, features + PARTS, BLOCK), BF16)], [],
        advertiser_vectors, spend_limits.reshape(1, BLOCK), params=None,
    )
    catalog = to_all(packed, IMP)

    exchange = [((n_imp, n_imp, BLOCK), F32), ((groups, GROUP), F32)]
    levels = [((n_imp, BLOCK), F32)]
    strips = [((n_imp + 1, STRIP, BLOCK), BF16)]
    sums = [((n_imp + 1, 8, BLOCK), F32), ((GROUP, 128), F32)]

    outlays, demand, rate = call(
        functools.partial(totals_kernel, True), 1, exchange + levels, strips + sums,
        work, catalog, viewers_t,
    )
    prices = jnp.zeros((n_imp, BLOCK), F32)
    duals = jnp.zeros((groups, GROUP), F32)

    def meet(outlays, demand, duals):
        outlays = to_all(outlays, IMP)
        pair = lax.all_gather(demand, ADV, axis=0, axis_index_groups=chip_groups())
        demand = lax.psum(
            (pair[0] + pair[1]).reshape(-1), ADV, axis_index_groups=ring_groups()
        ).reshape(demand.shape)
        duals = jnp.maximum(duals + demand / caps - 1.0, 0.0)
        return outlays, duals

    for _ in range(2):
        outlays, duals = meet(outlays, demand, duals)
        outlays, demand, prices = call(
            functools.partial(totals_kernel, False), 1, exchange + levels,
            strips + sums,
            work, catalog, viewers_t, outlays, prices, rate, duals,
        )
    outlays, duals = meet(outlays, demand, duals)
    adv_parts, own_prices, out_duals, strip_rows = call(
        adv_kernel, 2,
        [
            ((n_imp, features, BLOCK), BF16),
            ((1, BLOCK), F32),
            ((groups, GROUP), F32),
            *strips,
        ],
        [((n_imp + 1, features, BLOCK), F32)] + levels,
        work, own, catalog, viewers_t, impression_vectors, outlays, prices, rate, duals,
    )
    adv_parts = to_all(adv_parts, IMP)
    (imp_parts,) = call(
        imp_kernel, 1, [((2, groups // 2, features, GROUP), F32)],
        [((groups, features, GROUP), F32)],
        work, catalog, viewers_t, strip_rows, duals,
    )
    ring = ring_of(lax.axis_index(ADV))
    kept = lax.dynamic_index_in_dim(imp_parts, ring, 0, keepdims=False)
    given = lax.dynamic_index_in_dim(imp_parts, 1 - ring, 0, keepdims=False)
    given = lax.ppermute(given, ADV, [(a, a ^ 1) for a in range(n_adv)])
    imp_parts = (kept + given).astype(BF16)
    imp_parts = lax.all_to_all(imp_parts, ADV, 0, 0, tiled=True, axis_index_groups=ring_groups())
    impression_grad = jnp.sum(imp_parts.astype(F32), axis=0).astype(BF16)
    advertiser_grad = jnp.sum(adv_parts.astype(F32), axis=0).astype(BF16)
    return own_prices.reshape(-1), out_duals.reshape(-1), impression_grad, advertiser_grad


def solution(mesh):
    n_imp, n_adv = (mesh.shape[axis] for axis in ("imp", "adv"))
    chips = jax.sharding.Mesh(mesh.devices.reshape(n_imp // 4, 4, n_adv), IMP + (ADV,))
    return jax.shard_map(
        local,
        mesh=chips,
        in_specs=(
            P(None, IMP),
            P(None, IMP + (ADV,)),
            P(IMP + (ADV,)),
            P(IMP),
            P(IMP, ADV, None),
            P(IMP, ADV),
        ),
        out_specs=(P(IMP + (ADV,)), P(IMP), P(None, IMP + (ADV,)), P(None, IMP + (ADV,))),
        check_vma=False,
    )
```

```python
import functools

import jax
import jax.numpy as jnp
from jax import lax
from jax.experimental import pallas as pl
from jax.experimental.pallas import tpu as pltpu
from jax.sharding import PartitionSpec as P


GROUP = 128
BLOCK = 128
PARTS = 8
STRIP = 16
UNROLL = 24
DEAD = 1e30

F32 = jnp.float32
BF16 = jnp.bfloat16
IMP = ("z", "x")
ADV = "adv"
VMEM = pl.BlockSpec(memory_space=pltpu.VMEM)
SMEM = pl.BlockSpec(memory_space=pltpu.SMEM)
PARAMS = pltpu.CompilerParams(vmem_limit_bytes=16 << 20)


def parts_of(value):
    high = value.astype(BF16).astype(F32)
    rest = value - high
    middle = rest.astype(BF16).astype(F32)
    return high, middle, rest - middle


def rows_of(rows, count):
    place = lax.broadcasted_iota(jnp.int32, (count, rows[0].shape[1]), 0)
    stacked = jnp.zeros((count, rows[0].shape[1]), F32)
    for index, row in enumerate(rows):
        stacked = jnp.where(place == index, row, stacked)
    return stacked


def pack_kernel(vectors, spend, out):
    features = vectors.shape[0]
    columns = vectors[...]
    limits = rows_of(parts_of(spend[...]), PARTS).astype(BF16)
    for peer in range(out.shape[0]):
        out[peer, :features, :] = columns
        out[peer, features:, :] = limits


def new_prices(outlays, old_prices, rate):
    return jnp.maximum(old_prices[...] + jnp.sum(outlays[...], axis=0) * rate[...] - 1.0, 0.0)


def set_strips(strips, prices):
    blocks = strips.shape[0] - 1
    strips[...] = jnp.zeros_like(strips)
    dead = jnp.full((1, BLOCK), -DEAD, F32)
    strips[blocks, :, :] = rows_of([dead], STRIP).astype(BF16)
    if prices is not None:
        parts = parts_of(-prices)
        for block in range(blocks):
            rows = rows_of([part[block : block + 1, :] for part in parts], 8)
            rows = jnp.concatenate([rows, jnp.zeros((STRIP - 8, BLOCK), F32)], axis=0)
            strips[block, :, :] = rows.astype(BF16)


def turned_duals(duals, width):
    parts = parts_of(duals)
    above = jnp.zeros((width - 3 * duals.shape[0], GROUP), F32)
    return jnp.concatenate([above, *parts], axis=0).T.astype(BF16)


def pair_scores(index, work, catalog, strips, viewers_t, turned):
    features = catalog.shape[1] - PARTS
    last = catalog.shape[0] - 1
    group_no, first, second = (work[row, index] for row in range(3))
    viewer = viewers_t[pl.ds(pl.multiple_of(group_no * GROUP, GROUP), GROUP), :]
    vectors = jnp.concatenate(
        [
            catalog[jnp.minimum(first, last), :features, :],
            catalog[jnp.minimum(second, last), :features, :],
        ],
        axis=1,
    )
    rows = [vectors, jnp.concatenate([strips[first], strips[second]], axis=1)]
    if turned is None:
        viewer = viewer[:, : features + STRIP]
    else:
        viewer = viewer + turned
        groups = (viewers_t.shape[1] - features - STRIP) // 3
        place = lax.broadcasted_iota(jnp.int32, (groups, 2 * BLOCK), 0)
        rows += [jnp.where(place == group_no, -1.0, 0.0).astype(BF16)] * 3
    scores = jnp.dot(viewer, jnp.concatenate(rows, axis=0), preferred_element_type=F32)
    return scores, vectors, group_no, first, second


def for_pairs(work, unroll, body):
    def step(number, _):
        body([number * unroll + offset for offset in range(unroll)])
        return 0

    lax.fori_loop(0, lax.div(work[3, 0] + (unroll - 1), unroll), step, 0)


def totals_kernel(first_pass, work, catalog, viewers_t, *refs):
    features = catalog.shape[1] - PARTS
    turned = None
    if first_pass:
        outlay_out, demand_out, rate, strips, outlay_acc, demand_acc = refs
        limits = catalog[:, features:, :].astype(F32)
        rate[...] = 1.0 / jnp.sum(limits, axis=1)
        set_strips(strips, None)
    else:
        (outlays, old_prices, rate, duals,
         outlay_out, demand_out, prices, strips, outlay_acc, demand_acc) = refs
        prices[...] = new_prices(outlays, old_prices, rate)
        set_strips(strips, prices[...])
        turned = turned_duals(duals[...], viewers_t.shape[1])
    outlay_acc[...] = jnp.zeros_like(outlay_acc)
    demand_acc[...] = jnp.zeros_like(demand_acc)

    lane = lax.broadcasted_iota(jnp.int32, (GROUP, 128), 1)

    def pairs(indices):
        demand = demand_acc[...]
        scored = [pair_scores(i, work, catalog, strips, viewers_t, turned) for i in indices]
        for scores, _, group_no, first, second in scored:
            shares = jnp.clip(scores, 0.0, 1.0)
            total = jnp.sum(shares[:, :BLOCK] + shares[:, BLOCK:], axis=1, keepdims=True)
            demand = demand + jnp.where(lane == group_no, total, 0.0)
            folded = jnp.sum(shares.reshape(GROUP // 8, 8, 2 * BLOCK), axis=0)
            outlay_acc[first] += folded[:, :BLOCK]
            outlay_acc[second] += folded[:, BLOCK:]
        demand_acc[...] = demand

    for_pairs(work, UNROLL, pairs)
    demand_out[...] = demand_acc[...].T[: demand_out.shape[0], :]
    peers = outlay_out.shape[0]
    outlay = jnp.sum(outlay_acc[:peers], axis=1)
    for peer in range(peers):
        outlay_out[peer] = outlay


def adv_kernel(
    work, own, catalog, viewers_t, viewers, outlays, old_prices, rate, duals,
    adv_out, own_prices, duals_out, strips_out, adv_acc, prices,
):
    prices[...] = new_prices(outlays, old_prices, rate)
    own_prices[...] = prices[pl.ds(own[0], 1), :]
    duals_out[...] = duals[...]
    set_strips(strips_out, prices[...])
    turned = turned_duals(duals[...], viewers_t.shape[1])
    adv_acc[...] = jnp.zeros_like(adv_acc)

    def pairs(indices):
        scored = [pair_scores(i, work, catalog, strips_out, viewers_t, turned) for i in indices]
        weighed = [jnp.clip(one[0], 0.0, 1.0).astype(BF16) for one in scored]
        for weights, (_, _, group_no, first, second) in zip(weighed, scored):
            viewer = viewers[:, pl.ds(pl.multiple_of(group_no * GROUP, GROUP), GROUP)]
            terms = jnp.dot(viewer, weights, preferred_element_type=F32)
            adv_acc[first] += terms[:, :BLOCK]
            adv_acc[second] += terms[:, BLOCK:]

    for_pairs(work, UNROLL, pairs)
    adv_out[...] = (adv_acc[: adv_out.shape[0]] * (1.0 / GROUP)).astype(BF16)


def imp_kernel(work, catalog, viewers_t, strips, duals, imp_out, imp_acc):
    turned = turned_duals(duals[...], viewers_t.shape[1])
    imp_acc[...] = jnp.zeros_like(imp_acc)

    def pairs(indices):
        scored = [pair_scores(i, work, catalog, strips, viewers_t, turned) for i in indices]
        weighed = [jnp.clip(one[0], 0.0, 1.0).astype(BF16) for one in scored]
        for weights, (_, vectors, group_no, _, _) in zip(weighed, scored):
            imp_acc[group_no] += lax.dot_general(
                vectors, weights, (((1,), (1,)), ((), ())), preferred_element_type=F32
            )

    for_pairs(work, UNROLL, pairs)
    for group_no in range(imp_acc.shape[0]):
        imp_out[ring_of(group_no), group_no // 2 % 2, group_no // 4] = imp_acc[group_no]


def chip_groups():
    return [[a, a + 1] for a in range(0, lax.axis_size(ADV), 2)]


def ring_of(place):
    return (place // 2 + place + 1) % 2


def ring_groups():
    places = range(lax.axis_size(ADV))
    return [[place for place in places if ring_of(place) == ring] for ring in (0, 1)]


def last_groups():
    return [ring[parity::2] for ring in ring_groups() for parity in (0, 1)]


def swapped(value, index, pairs):
    kept = lax.dynamic_index_in_dim(value, index, 0, keepdims=False)
    given = lax.dynamic_index_in_dim(value, 1 - index, 0, keepdims=False)
    return kept + lax.ppermute(given, ADV, pairs)


def to_all(value, axis):
    return lax.all_to_all(value, axis, 0, 0, tiled=True)


def work_list(ids, counts, dead):
    _, slots = ids.shape
    ids = jnp.where(jnp.arange(slots)[None, :] < counts, ids, dead)
    live = (jnp.arange(0, slots, 2)[None, :] < counts).reshape(-1)
    pairs = jnp.arange(live.size)
    entries = jnp.arange(-(-live.size // UNROLL) * UNROLL)
    place = jnp.sum(live[None, :] & (pairs[None, :] < pairs[:, None]), axis=1)
    chosen = live[None, :] & (place[None, :] == entries[:, None])
    group_no = pairs // (slots // 2)
    rows = [
        jnp.sum(jnp.where(chosen, row[None, :] - rest, 0), axis=1) + rest
        for row, rest in ((group_no, 0), (ids[:, ::2].reshape(-1), dead), (ids[:, 1::2].reshape(-1), dead))
    ]
    rows.append(jnp.full_like(entries, jnp.sum(live)))
    return jnp.stack(rows).astype(jnp.int32)


def call(kernel, n_smem, out_shape, scratch, *args, params=PARAMS):
    return pl.pallas_call(
        kernel,
        in_specs=[SMEM] * n_smem + [VMEM] * (len(args) - n_smem),
        out_specs=(VMEM,) * len(out_shape),
        out_shape=tuple(jax.ShapeDtypeStruct(shape, dtype) for shape, dtype in out_shape),
        scratch_shapes=[pltpu.VMEM(shape, dtype) for shape, dtype in scratch],
        compiler_params=params,
    )(*args)


def local(impression_vectors, advertiser_vectors, spend_limits, capacity, blocks, counts):
    features = impression_vectors.shape[0]
    groups, _, slots = blocks.shape
    n_imp, n_adv = lax.axis_size(IMP), lax.axis_size(ADV)
    work = work_list(blocks.reshape(groups, slots) // n_adv, counts, n_imp)
    own = lax.axis_index(IMP).astype(jnp.int32).reshape(1)
    caps = capacity.reshape(groups, GROUP)
    ones = jnp.ones((3, impression_vectors.shape[1]), BF16)
    rest = STRIP - 3 + 3 * groups
    zeros = jnp.zeros((rest, impression_vectors.shape[1]), BF16)
    viewers_t = jnp.concatenate([impression_vectors, ones, zeros], axis=0).T

    (packed,) = call(
        pack_kernel, 0, [((n_imp, features + PARTS, BLOCK), BF16)], [],
        advertiser_vectors, spend_limits.reshape(1, BLOCK), params=None,
    )
    catalog = to_all(packed, IMP)

    exchange = [((n_imp, n_imp, BLOCK), F32), ((groups, GROUP), F32)]
    levels = [((n_imp, BLOCK), F32)]
    strips = [((n_imp + 1, STRIP, BLOCK), BF16)]
    sums = [((n_imp + 1, 8, BLOCK), F32), ((GROUP, 128), F32)]

    outlays, demand, rate = call(
        functools.partial(totals_kernel, True), 1, exchange + levels, strips + sums,
        work, catalog, viewers_t,
    )
    prices = jnp.zeros((n_imp, BLOCK), F32)
    duals = jnp.zeros((groups, GROUP), F32)

    def meet(outlays, demand, duals):
        outlays = to_all(outlays, IMP)
        pair = lax.all_gather(demand, ADV, axis=0, axis_index_groups=chip_groups())
        demand = lax.psum(
            (pair[0] + pair[1]).reshape(-1), ADV, axis_index_groups=ring_groups()
        ).reshape(demand.shape)
        duals = jnp.maximum(duals + demand / caps - 1.0, 0.0)
        return outlays, duals

    for _ in range(2):
        outlays, duals = meet(outlays, demand, duals)
        outlays, demand, prices = call(
            functools.partial(totals_kernel, False), 1, exchange + levels,
            strips + sums,
            work, catalog, viewers_t, outlays, prices, rate, duals,
        )
    outlays, duals = meet(outlays, demand, duals)
    adv_parts, own_prices, out_duals, strip_rows = call(
        adv_kernel, 2,
        [
            ((n_imp, features, BLOCK), BF16),
            ((1, BLOCK), F32),
            ((groups, GROUP), F32),
            *strips,
        ],
        [((n_imp + 1, features, BLOCK), F32)] + levels,
        work, own, catalog, viewers_t, impression_vectors, outlays, prices, rate, duals,
    )
    adv_parts = to_all(adv_parts, IMP)
    (imp_parts,) = call(
        imp_kernel, 1, [((2, 2, groups // 4, features, GROUP), F32)],
        [((groups, features, GROUP), F32)],
        work, catalog, viewers_t, strip_rows, duals,
    )
    place = lax.axis_index(ADV)
    rings = ring_groups()
    next_chip = [(ring[y], ring[y ^ 1]) for ring in rings for y in range(n_adv // 2)]
    imp_parts = swapped(imp_parts, ring_of(place), [(a, a ^ 1) for a in range(n_adv)])
    imp_parts = swapped(imp_parts, place // 2 % 2, next_chip).astype(BF16)
    imp_parts = lax.all_to_all(imp_parts, ADV, 0, 0, tiled=True, axis_index_groups=last_groups())
    impression_grad = jnp.sum(imp_parts.astype(F32), axis=0).astype(BF16)
    advertiser_grad = jnp.sum(adv_parts.astype(F32), axis=0).astype(BF16)
    return own_prices.reshape(-1), out_duals.reshape(-1), impression_grad, advertiser_grad


def solution(mesh):
    n_imp, n_adv = (mesh.shape[axis] for axis in ("imp", "adv"))
    chips = jax.sharding.Mesh(mesh.devices.reshape(n_imp // 4, 4, n_adv), IMP + (ADV,))
    return jax.shard_map(
        local,
        mesh=chips,
        in_specs=(
            P(None, IMP),
            P(None, IMP + (ADV,)),
            P(IMP + (ADV,)),
            P(IMP),
            P(IMP, ADV, None),
            P(IMP, ADV),
        ),
        out_specs=(P(IMP + (ADV,)), P(IMP), P(None, IMP + (ADV,)), P(None, IMP + (ADV,))),
        check_vma=False,
    )
```

```python
import functools

import jax
import jax.numpy as jnp
from jax import lax
from jax.experimental import pallas as pl
from jax.experimental.pallas import tpu as pltpu
from jax.sharding import PartitionSpec as P


GROUP = 128
BLOCK = 128
PARTS = 8
STRIP = 16
UNROLL = 22
DEAD = 1e30

F32 = jnp.float32
BF16 = jnp.bfloat16
IMP = "imp"
ROW = 4
ADV = "adv"
VMEM = pl.BlockSpec(memory_space=pltpu.VMEM)
SMEM = pl.BlockSpec(memory_space=pltpu.SMEM)
PARAMS = pltpu.CompilerParams(vmem_limit_bytes=16 << 20)


def parts_of(value):
    high = value.astype(BF16).astype(F32)
    rest = value - high
    middle = rest.astype(BF16).astype(F32)
    return high, middle, rest - middle


def rows_of(rows, count):
    place = lax.broadcasted_iota(jnp.int32, (count, rows[0].shape[1]), 0)
    stacked = jnp.zeros((count, rows[0].shape[1]), F32)
    for index, row in enumerate(rows):
        stacked = jnp.where(place == index, row, stacked)
    return stacked


def pack_kernel(vectors, spend, out):
    features = vectors.shape[0]
    columns = vectors[...]
    limits = rows_of(parts_of(spend[...]), PARTS).astype(BF16)
    for peer in range(out.shape[0]):
        out[peer, :features, :] = columns
        out[peer, features:, :] = limits


def new_prices(outlays, old_prices, rate):
    return jnp.maximum(old_prices[...] + jnp.sum(outlays[...], axis=0) * rate[...] - 1.0, 0.0)


def set_strips(strips, prices):
    blocks = strips.shape[0] - 1
    strips[...] = jnp.zeros_like(strips)
    dead = jnp.full((1, BLOCK), -DEAD, F32)
    strips[blocks, :, :] = rows_of([dead], STRIP).astype(BF16)
    if prices is not None:
        parts = parts_of(-prices)
        for block in range(blocks):
            rows = rows_of([part[block : block + 1, :] for part in parts], 8)
            rows = jnp.concatenate([rows, jnp.zeros((STRIP - 8, BLOCK), F32)], axis=0)
            strips[block, :, :] = rows.astype(BF16)


def turned_duals(duals, width):
    parts = parts_of(duals)
    above = jnp.zeros((width - 3 * duals.shape[0], GROUP), F32)
    return jnp.concatenate([above, *parts], axis=0).T.astype(BF16)


def pair_scores(index, work, catalog, strips, viewers_t, turned):
    features = catalog.shape[1] - PARTS
    last = catalog.shape[0] - 1
    group_no, first, second = (work[row, index] for row in range(3))
    viewer = viewers_t[pl.ds(pl.multiple_of(group_no * GROUP, GROUP), GROUP), :]
    vectors = jnp.concatenate(
        [
            catalog[jnp.minimum(first, last), :features, :],
            catalog[jnp.minimum(second, last), :features, :],
        ],
        axis=1,
    )
    rows = [vectors, jnp.concatenate([strips[first], strips[second]], axis=1)]
    if turned is None:
        viewer = viewer[:, : features + STRIP]
    else:
        viewer = viewer + turned
        groups = (viewers_t.shape[1] - features - STRIP) // 3
        place = lax.broadcasted_iota(jnp.int32, (groups, 2 * BLOCK), 0)
        rows += [jnp.where(place == group_no, -1.0, 0.0).astype(BF16)] * 3
    scores = jnp.dot(viewer, jnp.concatenate(rows, axis=0), preferred_element_type=F32)
    return scores, vectors, group_no, first, second


def for_pairs(work, unroll, body):
    def step(number, _):
        body([number * unroll + offset for offset in range(unroll)])
        return 0

    lax.fori_loop(0, lax.div(work[3, 0] + (unroll - 1), unroll), step, 0)


def totals_kernel(first_pass, work, catalog, viewers_t, *refs):
    features = catalog.shape[1] - PARTS
    turned = None
    if first_pass:
        outlay_out, demand_out, rate, strips, outlay_acc, demand_acc = refs
        limits = catalog[:, features:, :].astype(F32)
        rate[...] = 1.0 / jnp.sum(limits, axis=1)
        set_strips(strips, None)
    else:
        (outlays, old_prices, rate, duals,
         outlay_out, demand_out, prices, strips, outlay_acc, demand_acc) = refs
        prices[...] = new_prices(outlays, old_prices, rate)
        set_strips(strips, prices[...])
        turned = turned_duals(duals[...], viewers_t.shape[1])
    outlay_acc[...] = jnp.zeros_like(outlay_acc)
    demand_acc[...] = jnp.zeros_like(demand_acc)

    lane = lax.broadcasted_iota(jnp.int32, (GROUP, 128), 1)

    def pairs(indices):
        demand = demand_acc[...]
        scored = [pair_scores(i, work, catalog, strips, viewers_t, turned) for i in indices]
        for scores, _, group_no, first, second in scored:
            shares = jnp.clip(scores, 0.0, 1.0)
            total = jnp.sum(shares[:, :BLOCK] + shares[:, BLOCK:], axis=1, keepdims=True)
            demand = demand + jnp.where(lane == group_no, total, 0.0)
            folded = jnp.sum(shares.reshape(GROUP // 8, 8, 2 * BLOCK), axis=0)
            outlay_acc[first] += folded[:, :BLOCK]
            outlay_acc[second] += folded[:, BLOCK:]
        demand_acc[...] = demand

    for_pairs(work, UNROLL, pairs)
    demand_out[...] = demand_acc[...].T[: demand_out.shape[0], :]
    peers = outlay_out.shape[0]
    outlay = jnp.sum(outlay_acc[:peers], axis=1)
    for peer in range(peers):
        outlay_out[peer] = outlay


def adv_kernel(
    work, own, catalog, viewers_t, viewers, outlays, old_prices, rate, duals,
    adv_out, own_prices, duals_out, strips_out, adv_acc, prices,
):
    prices[...] = new_prices(outlays, old_prices, rate)
    own_prices[...] = prices[pl.ds(own[0], 1), :]
    duals_out[...] = duals[...]
    set_strips(strips_out, prices[...])
    turned = turned_duals(duals[...], viewers_t.shape[1])
    adv_acc[...] = jnp.zeros_like(adv_acc)

    def pairs(indices):
        scored = [pair_scores(i, work, catalog, strips_out, viewers_t, turned) for i in indices]
        weighed = [jnp.clip(one[0], 0.0, 1.0).astype(BF16) for one in scored]
        for weights, (_, _, group_no, first, second) in zip(weighed, scored):
            viewer = viewers[:, pl.ds(pl.multiple_of(group_no * GROUP, GROUP), GROUP)]
            terms = jnp.dot(viewer, weights, preferred_element_type=F32)
            adv_acc[first] += terms[:, :BLOCK]
            adv_acc[second] += terms[:, BLOCK:]

    for_pairs(work, UNROLL, pairs)
    adv_out[...] = (adv_acc[: adv_out.shape[0]] * (1.0 / GROUP)).astype(BF16)


def imp_kernel(work, catalog, viewers_t, strips, duals, imp_out, imp_acc):
    turned = turned_duals(duals[...], viewers_t.shape[1])
    imp_acc[...] = jnp.zeros_like(imp_acc)

    def pairs(indices):
        scored = [pair_scores(i, work, catalog, strips, viewers_t, turned) for i in indices]
        weighed = [jnp.clip(one[0], 0.0, 1.0).astype(BF16) for one in scored]
        for weights, (_, vectors, group_no, _, _) in zip(weighed, scored):
            imp_acc[group_no] += lax.dot_general(
                vectors, weights, (((1,), (1,)), ((), ())), preferred_element_type=F32
            )

    for_pairs(work, UNROLL, pairs)
    for group_no in range(imp_acc.shape[0]):
        imp_out[ring_of(group_no), group_no // 2 % 2, group_no // 4] = imp_acc[group_no]


def chip_groups():
    return [[a, a + 1] for a in range(0, lax.axis_size(ADV), 2)]


def ring_of(place):
    return (place // 2 + place + 1) % 2


def ring_groups():
    places = range(lax.axis_size(ADV))
    return [[place for place in places if ring_of(place) == ring] for ring in (0, 1)]


def last_groups():
    return [ring[parity::2] for ring in ring_groups() for parity in (0, 1)]


def swapped(value, index, pairs):
    kept = lax.dynamic_index_in_dim(value, index, 0, keepdims=False)
    given = lax.dynamic_index_in_dim(value, 1 - index, 0, keepdims=False)
    return kept + lax.ppermute(given, ADV, pairs)


def snake(index):
    row, place = index // ROW, index % ROW
    return row * ROW + place + row % 2 * (ROW - 1 - 2 * place)


def to_peers(value):
    order = [snake(index) for index in range(lax.axis_size(IMP))]
    return lax.all_to_all(value, IMP, 0, 0, tiled=True, axis_index_groups=[order])


def work_list(ids, counts, dead):
    _, slots = ids.shape
    ids = jnp.where(jnp.arange(slots)[None, :] < counts, ids, dead)
    live = (jnp.arange(0, slots, 2)[None, :] < counts).reshape(-1)
    pairs = jnp.arange(live.size)
    entries = jnp.arange(-(-live.size // UNROLL) * UNROLL)
    place = jnp.sum(live[None, :] & (pairs[None, :] < pairs[:, None]), axis=1)
    chosen = live[None, :] & (place[None, :] == entries[:, None])
    group_no = pairs // (slots // 2)
    rows = [
        jnp.sum(jnp.where(chosen, row[None, :] - rest, 0), axis=1) + rest
        for row, rest in ((group_no, 0), (ids[:, ::2].reshape(-1), dead), (ids[:, 1::2].reshape(-1), dead))
    ]
    rows.append(jnp.full_like(entries, jnp.sum(live)))
    return jnp.stack(rows).astype(jnp.int32)


def call(kernel, n_smem, out_shape, scratch, *args, params=PARAMS):
    return pl.pallas_call(
        kernel,
        in_specs=[SMEM] * n_smem + [VMEM] * (len(args) - n_smem),
        out_specs=(VMEM,) * len(out_shape),
        out_shape=tuple(jax.ShapeDtypeStruct(shape, dtype) for shape, dtype in out_shape),
        scratch_shapes=[pltpu.VMEM(shape, dtype) for shape, dtype in scratch],
        compiler_params=params,
    )(*args)


def local(impression_vectors, advertiser_vectors, spend_limits, capacity, blocks, counts):
    features = impression_vectors.shape[0]
    groups, _, slots = blocks.shape
    n_imp, n_adv = lax.axis_size(IMP), lax.axis_size(ADV)
    work = work_list(snake(blocks.reshape(groups, slots) // n_adv), counts, n_imp)
    own = snake(lax.axis_index(IMP)).astype(jnp.int32).reshape(1)
    caps = capacity.reshape(groups, GROUP)
    ones = jnp.ones((3, impression_vectors.shape[1]), BF16)
    rest = STRIP - 3 + 3 * groups
    zeros = jnp.zeros((rest, impression_vectors.shape[1]), BF16)
    viewers_t = jnp.concatenate([impression_vectors, ones, zeros], axis=0).T

    (packed,) = call(
        pack_kernel, 0, [((n_imp, features + PARTS, BLOCK), BF16)], [],
        advertiser_vectors, spend_limits.reshape(1, BLOCK), params=None,
    )
    catalog = to_peers(packed)

    exchange = [((n_imp, n_imp, BLOCK), F32), ((groups, GROUP), F32)]
    levels = [((n_imp, BLOCK), F32)]
    strips = [((n_imp + 1, STRIP, BLOCK), BF16)]
    sums = [((n_imp + 1, 8, BLOCK), F32), ((GROUP, 128), F32)]

    outlays, demand, rate = call(
        functools.partial(totals_kernel, True), 1, exchange + levels, strips + sums,
        work, catalog, viewers_t,
    )
    prices = jnp.zeros((n_imp, BLOCK), F32)
    duals = jnp.zeros((groups, GROUP), F32)

    def meet(outlays, demand, duals):
        outlays = to_peers(outlays)
        pair = lax.all_gather(demand, ADV, axis=0, axis_index_groups=chip_groups())
        demand = lax.psum(
            (pair[0] + pair[1]).reshape(-1), ADV, axis_index_groups=ring_groups()
        ).reshape(demand.shape)
        duals = jnp.maximum(duals + demand / caps - 1.0, 0.0)
        return outlays, duals

    for _ in range(2):
        outlays, duals = meet(outlays, demand, duals)
        outlays, demand, prices = call(
            functools.partial(totals_kernel, False), 1, exchange + levels,
            strips + sums,
            work, catalog, viewers_t, outlays, prices, rate, duals,
        )
    outlays, duals = meet(outlays, demand, duals)
    adv_parts, own_prices, out_duals, strip_rows = call(
        adv_kernel, 2,
        [
            ((n_imp, features, BLOCK), BF16),
            ((1, BLOCK), F32),
            ((groups, GROUP), F32),
            *strips,
        ],
        [((n_imp + 1, features, BLOCK), F32)] + levels,
        work, own, catalog, viewers_t, impression_vectors, outlays, prices, rate, duals,
    )
    adv_parts = to_peers(adv_parts)
    (imp_parts,) = call(
        imp_kernel, 1, [((2, 2, groups // 4, features, GROUP), F32)],
        [((groups, features, GROUP), F32)],
        work, catalog, viewers_t, strip_rows, duals,
    )
    place = lax.axis_index(ADV)
    rings = ring_groups()
    next_chip = [(ring[y], ring[y ^ 1]) for ring in rings for y in range(n_adv // 2)]
    imp_parts = swapped(imp_parts, ring_of(place), [(a, a ^ 1) for a in range(n_adv)])
    imp_parts = swapped(imp_parts, place // 2 % 2, next_chip).astype(BF16)
    imp_parts = lax.all_to_all(imp_parts, ADV, 0, 0, tiled=True, axis_index_groups=last_groups())
    impression_grad = jnp.sum(imp_parts.astype(F32), axis=0).astype(BF16)
    advertiser_grad = jnp.sum(adv_parts.astype(F32), axis=0).astype(BF16)
    return own_prices.reshape(-1), out_duals.reshape(-1), impression_grad, advertiser_grad


def solution(mesh):
    return jax.shard_map(
        local,
        mesh=mesh,
        in_specs=(
            P(None, IMP),
            P(None, (IMP, ADV)),
            P((IMP, ADV)),
            P(IMP),
            P(IMP, ADV, None),
            P(IMP, ADV),
        ),
        out_specs=(P((IMP, ADV)), P(IMP), P(None, (IMP, ADV)), P(None, (IMP, ADV))),
        check_vma=False,
    )
```
